128 devices in a mesh: row: 8 (over y, core), col: 8 (over x, z_lo), half: 2 (over z_hi).
Axes of the slice: x: 4, y: 4, z: 4 (z_hi: 2, z_lo: 2; z = z_hi * 2 + z_lo), core: 2. Of those that a mesh axis runs over, the one named last changes fastest.
Arguments:
- dosages: float32 [32768, 1024], P(('row', 'col', 'half')), may hold values from 0 to 2, as said below
- called_mask: int32 [32768, 1024], P(('row', 'col', 'half')), may hold values from 0 to 1, as said below
Outputs:
- relationship: bfloat16 [32768, 8, 8, 2, 256], P('row', None, 'col', 'half')
The draws below stay inside these ranges and needn't reach their ends.
Inputs may be any that keep to these rules, and one draw needn't show every extreme that they name: dosages are imputed expected allele counts of a diploid sample, the sum of two haplotype dosages each between 0 and 1. `called_mask`: an allele column may have no called sample at all.
All inputs are finite; a program needn't handle non-finite values.
Results may differ from the reference program's by a relative error of at most 0.0085.
Values may be sent and summed in bfloat16 or wider, within the bound.
No kernel may reach another device: no remote copies, remote signals or barrier semaphores. Data moves between devices by JAX's collectives and lax.ppermute only.
A program may use at most 128 MiB of HBM per device.

```python
import jax
import jax.numpy as jnp
from jax import lax

M = 1024
SD = 256
N = 32768
BLOCK = 4096
N_ROW = 8
N_COL = 8
N_HALF = 2


def draw_dosages(key, part):
    key_rate = jax.random.fold_in(key, 11)
    key_first = jax.random.fold_in(key, 12)
    key_second = jax.random.fold_in(key, 13)
    key_sure = jax.random.fold_in(key, 14)
    key_noise_one = jax.random.fold_in(key, 15)
    key_noise_two = jax.random.fold_in(key, 16)
    threshold = jax.random.randint(key_rate, (1, M), 4, 1001)
    first = jax.random.randint(key_first, (N, M), 0, 2000)
    second = jax.random.randint(key_second, (N, M), 0, 2000)
    sure = jax.random.randint(key_sure, (N, M), 0, 4)
    noise_one = jnp.abs(jax.random.normal(key_noise_one, (N, M), jnp.float32)) * 0.15
    noise_two = jnp.abs(jax.random.normal(key_noise_two, (N, M), jnp.float32)) * 0.15
    noise_one = jnp.minimum(noise_one, 0.49)
    noise_two = jnp.minimum(noise_two, 0.49)
    keep = jnp.where(sure == 0, 0.0, 1.0).astype(jnp.float32)
    noise_one = noise_one * keep
    noise_two = noise_two * keep
    haplo_one = jnp.where(first < threshold, 1.0 - noise_one, noise_one)
    haplo_two = jnp.where(second < threshold, 1.0 - noise_two, noise_two)
    return (haplo_one + haplo_two).astype(jnp.float32)


def draw_called_mask(key, part):
    key_cells = jax.random.fold_in(key, 21)
    key_columns = jax.random.fold_in(key, 22)
    key_forced = jax.random.fold_in(key, 23)
    cells = jax.random.randint(key_cells, (N, M), 0, 10)
    column_pick = jax.random.randint(key_columns, (1, M), 0, 32)
    forced = jax.random.randint(key_forced, (), 0, M)
    column_index = jnp.arange(M, dtype=jnp.int32).reshape(1, M)
    dead = (column_pick == 0) | (column_index == forced)
    live = jnp.where(dead, 0, 1).astype(jnp.int32)
    return (cells < 9).astype(jnp.int32) * live


def setup_inputs(seed: int = 0) -> dict:
    key_list = jax.random.split(jax.random.key(seed), 3)
    return {
        "dosages": draw_dosages(jax.random.fold_in(key_list[2], 71), 0),
        "called_mask": draw_called_mask(jax.random.fold_in(key_list[2], 71), 0),
    }


def standardize(dosages, called_mask):
    called = called_mask.astype(jnp.float32)
    values = dosages.astype(jnp.float32)
    allele_sum = lax.optimization_barrier(jnp.sum(called * values, axis=0))
    called_count = lax.optimization_barrier(jnp.sum(called, axis=0))
    frequency = allele_sum / (2.0 * jnp.maximum(called_count, 1.0))
    spread = jnp.maximum(2.0 * frequency * (1.0 - frequency), 0.05)
    return (called * (values - 2.0 * frequency) * lax.rsqrt(spread)).astype(jnp.bfloat16)

def reference(dosages, called_mask):
    standard = standardize(dosages, called_mask)
    width = M // N_HALF
    blocks = standard.reshape(N_ROW, BLOCK, M)

    def one_block(rows_block):
        total = jnp.zeros((BLOCK, N), jnp.float32)
        for section in range(N_HALF):
            lower = section * width
            product = lax.dot_general(rows_block[:, lower:lower + width], standard[:, lower:lower + width], (((1,), (1,)), ((), ())), preferred_element_type=jnp.float32) / M
            total = total + product.astype(jnp.bfloat16).astype(jnp.float32)
        return total.astype(jnp.bfloat16)
    result = lax.map(one_block, blocks)
    return result.reshape(N, N_ROW, N_COL, N_HALF, SD)
```

```python
import functools

import jax
import jax.numpy as jnp
import numpy as np
from jax import lax
from jax.experimental import pallas as pl
from jax.experimental.pallas import tpu as pltpu
from jax.sharding import Mesh
from jax.sharding import PartitionSpec as P


M = 1024
SD = 256
N_ROW = 8
SHARES = 16
ALL = ("row_0", "row_1", "col_0", "col_1", "half")
X = "col_0"
Y = "row_0"
CORE = "row_1"
Z = ("col_1", "half")
Z_INDEX = (0, 2, 1, 3)


def shift(value, axis, step):
    place = Z_INDEX if axis == Z else range(4)
    return lax.ppermute(value, axis, [(place[i], place[(i + step) % 4]) for i in range(4)])


def swap(value):
    return lax.ppermute(value, CORE, [(0, 1), (1, 0)])


def ring_sum(value, axis):
    after, before, across = shift(value, axis, -1), shift(value, axis, 1), shift(value, axis, 2)
    return (value + across) + (after + before)


def places(plane, line):
    table = np.zeros((4, 2, 4, 2, 2, SHARES + N_ROW), np.int32)
    for y, core, x, low, high in np.ndindex(table.shape[:-1]):
        z = high * 2 + low
        rows = [((x + dx) % 4, (z + dz) % 4) for dx, dz in plane]
        columns = [((y + dy) % 4, (core + dc) % 2) for dy, dc in line]
        table[y, core, x, low, high] = [(i * 2 + k % 2) * 2 + k // 2 for i, k in rows] + [
            j * 2 + c for j, c in columns
        ]
    return table.reshape(-1, SHARES + N_ROW)


def product_kernel(place, *refs, first, count, fresh):
    panels = refs[:count]
    pieces = refs[count : count + N_ROW]
    out = refs[count + N_ROW + (0 if fresh else 1)]
    panel_buf, piece_buf, wide, panel_sem, piece_sem = refs[count + N_ROW + (1 if fresh else 2) :]
    step = pl.program_id(0)

    def panel_copy(which, slot):
        return pltpu.make_async_copy(panels[which], panel_buf.at[slot], panel_sem.at[slot])

    def piece_copy(which):
        at = pl.multiple_of(place[SHARES + which] * SD, SD)
        return pltpu.make_async_copy(
            pieces[which], piece_buf.at[pl.ds(at, SD), :], piece_sem.at[which]
        )

    @pl.when(step == 0)
    def _():
        panel_copy(0, 0).start()
        for which in range(N_ROW):
            piece_copy(which).start()

    for which in range(1, count):

        @pl.when(step == which - 1)
        def _(which=which):
            panel_copy(which, which % 2).start()

    slot = step % 2
    panel_copy(0, slot).wait()

    @pl.when(step == 0)
    def _():
        for which in range(N_ROW):
            piece_copy(which).wait()

    left = panel_buf[slot]
    for a in range(N_ROW):
        part = lax.dot_general(
            left,
            piece_buf[a * SD : (a + 1) * SD, :],
            (((1,), (1,)), ((), ())),
            preferred_element_type=jnp.float32,
        ) * (1.0 / M)
        wide[0, pl.ds(a, SD, stride=N_ROW), :] = part[:, :128]
        wide[1, pl.ds(a, SD, stride=N_ROW), :] = part[:, 128:]
    out[:, :, :128] = wide[0].reshape(SD, N_ROW, 128).astype(jnp.bfloat16)
    out[:, :, 128:] = wide[1].reshape(SD, N_ROW, 128).astype(jnp.bfloat16)


def products(shares, first, last, pieces, place, previous):
    panels = shares[first:last]
    count = last - first
    fresh = previous is None
    anywhere = pl.BlockSpec(memory_space=pl.ANY)
    return pl.pallas_call(
        functools.partial(product_kernel, first=first, count=count, fresh=fresh),
        grid_spec=pltpu.PrefetchScalarGridSpec(
            num_scalar_prefetch=1,
            grid=(count,),
            in_specs=[anywhere] * (count + N_ROW + (0 if fresh else 1)),
            out_specs=pl.BlockSpec((SD, N_ROW, SD), lambda i, place: (place[first + i], 0, 0)),
            scratch_shapes=[
                pltpu.VMEM((2, SD, M), jnp.bfloat16),
                pltpu.VMEM((N_ROW * SD, M), jnp.bfloat16),
                pltpu.VMEM((2, SD * N_ROW, 128), jnp.float32),
                pltpu.SemaphoreType.DMA((2,)),
                pltpu.SemaphoreType.DMA((N_ROW,)),
            ],
        ),
        out_shape=jax.ShapeDtypeStruct((SHARES * SD, N_ROW, SD), jnp.bfloat16),
        input_output_aliases={} if fresh else {1 + count + N_ROW: 0},
        compiler_params=pltpu.CompilerParams(vmem_limit_bytes=24 << 20),
        cost_estimate=pl.CostEstimate(
            flops=2 * count * SD * N_ROW * SD * M,
            bytes_accessed=2 * (count * SD * (M + N_ROW * SD) + N_ROW * SD * M),
            transcendentals=0,
        ),
    )(place, *panels, *pieces, *([] if fresh else [previous]))


def shards(dosages, called_mask):
    called = called_mask.astype(jnp.float32)
    sums = jnp.stack([jnp.sum(called * dosages, axis=0), jnp.sum(called, axis=0)])
    sums = sums + swap(sums)
    for axis in (Y, X, Z):
        sums = ring_sum(sums, axis)
    frequency = sums[0] / (2.0 * jnp.maximum(sums[1], 1.0))
    spread = jnp.maximum(2.0 * frequency * (1.0 - frequency), 0.05)
    own = (called * (dosages - 2.0 * frequency) * lax.rsqrt(spread)).astype(jnp.bfloat16)

    line = {(0, 0): own}
    line[-1, 0] = shift(own, Y, 1)
    line[1, 0] = shift(own, Y, -1)
    line[2, 0] = shift(line[-1, 0], Y, 1)
    for step in (0, -1, 1, 2):
        line[step, 1] = swap(line[step, 0])
    pieces = list(line.values())

    plane = {(0, 0): own}

    def forward(source, axis, step):
        dx, dz = source
        target = (dx - step, dz) if axis == X else (dx, dz - step)
        plane[target] = shift(plane[source], axis, step)

    for source, axis, step in (
        ((0, 0), X, 1),
        ((0, 0), X, -1),
        ((0, 0), Z, 1),
        ((0, 0), Z, -1),
        ((0, -1), X, 1),
        ((0, 1), X, -1),
        ((1, 0), Z, 1),
        ((-1, 0), Z, -1),
        ((-1, -1), X, 1),
        ((1, 1), X, -1),
        ((1, -1), Z, 1),
        ((-1, 1), Z, -1),
        ((-1, 0), X, 1),
        ((0, -1), Z, 1),
        ((1, -2), X, -1),
    ):
        forward(source, axis, step)
    shares = list(plane.values())
    place = lax.dynamic_index_in_dim(
        jnp.asarray(places(list(plane), list(line))), lax.axis_index(ALL), keepdims=False
    )

    total = None
    for first, last in ((0, 9), (9, 13), (13, 16)):
        total = products(shares, first, last, pieces, place, total)
    return total.reshape(total.shape[0], N_ROW, 1, 1, SD)


def solution(mesh):
    torus = Mesh(mesh.devices.reshape(4, 2, 4, 2, mesh.shape["half"]), ALL)
    return jax.shard_map(
        shards,
        mesh=torus,
        in_specs=(P(ALL, None), P(ALL, None)),
        out_specs=P(("row_0", "row_1"), None, ("col_0", "col_1"), "half", None),
        check_vma=False,
    )
```

```python
import functools

import jax
import jax.numpy as jnp
import numpy as np
from jax import lax
from jax.experimental import pallas as pl
from jax.experimental.pallas import tpu as pltpu
from jax.sharding import Mesh
from jax.sharding import PartitionSpec as P


M = 1024
SD = 256
N_ROW = 8
SHARES = 16
WIDTH = 256
ROWS = SD + 8
CALLED_ZERO = 2.0**-100
ALL = ("row_0", "row_1", "col_0", "col_1", "half")
X = "col_0"
Y = "row_0"
CORE = "row_1"
Z = ("col_1", "half")
Z_INDEX = (0, 2, 1, 3)


def shift(value, axis, step):
    place = Z_INDEX if axis == Z else range(4)
    return lax.ppermute(value, axis, [(place[i], place[(i + step) % 4]) for i in range(4)])


def swap(value):
    return lax.ppermute(value, CORE, [(0, 1), (1, 0)])


def across(before, after):
    pairs = [(y * 2, (y + 1) % 4 * 2) for y in range(4)]
    pairs += [(y * 2 + 1, (y - 1) % 4 * 2 + 1) for y in range(4)]
    value = jnp.where(lax.axis_index(CORE) == 0, before, after)
    return lax.ppermute(value, (Y, CORE), pairs)


def ring_sum(value, axis):
    place = Z_INDEX if axis == Z else range(4)
    for partner in ((1, 0, 3, 2), (3, 2, 1, 0)):
        other = lax.ppermute(value, axis, [(place[j], place[partner[j]]) for j in range(4)])
        value = value + other
    return value


def places(plane, line):
    table = np.zeros((4, 2, 4, 2, 2, SHARES + N_ROW), np.int32)
    for y, core, x, low, high in np.ndindex(table.shape[:-1]):
        z = high * 2 + low
        rows = [((x + dx) % 4, (z + dz) % 4) for dx, dz in plane]
        columns = [((y + dy) % 4, (core + dc) % 2) for dy, dc in line]
        table[y, core, x, low, high] = [(i * 2 + k % 2) * 2 + k // 2 for i, k in rows] + [
            j * 2 + c for j, c in columns
        ]
    return table.reshape(-1, SHARES + N_ROW)


def centre_kernel(dosages, called_mask, shard, sums, dose_buf, mask_buf, sem):
    def copies(part):
        at = pl.ds(part * WIDTH, WIDTH)
        return (
            pltpu.make_async_copy(dosages.at[:, at], dose_buf.at[part], sem.at[0, part]),
            pltpu.make_async_copy(called_mask.at[:, at], mask_buf.at[part], sem.at[1, part]),
        )

    for part in range(M // WIDTH):
        for copy in copies(part):
            copy.start()
    for part in range(M // WIDTH):
        for copy in copies(part):
            copy.wait()
        at = slice(part * WIDTH, (part + 1) * WIDTH)
        dose = dose_buf[part]
        called = mask_buf[part] != 0
        total = jnp.sum(jnp.where(called, dose, 0.0), axis=0, keepdims=True)
        count = jnp.sum(jnp.where(called, 1.0, 0.0), axis=0, keepdims=True)
        centre = (total / jnp.maximum(count, 1.0)).astype(jnp.bfloat16).astype(jnp.float32)
        away = (dose - centre).astype(jnp.bfloat16).astype(jnp.float32)
        away = jnp.where(away == 0.0, CALLED_ZERO, away)
        shard[:SD, at] = jnp.where(called, away, 0.0).astype(jnp.bfloat16)
        shard[SD:, at] = jnp.broadcast_to(centre, (8, WIDTH)).astype(jnp.bfloat16)
        sums[0:1, at] = total
        sums[1:2, at] = count


def centred(dosages, called_mask):
    return pl.pallas_call(
        centre_kernel,
        in_specs=[pl.BlockSpec(memory_space=pltpu.HBM)] * 2,
        out_specs=[pl.BlockSpec(memory_space=pltpu.VMEM)] * 2,
        out_shape=[
            jax.ShapeDtypeStruct((ROWS, M), jnp.bfloat16),
            jax.ShapeDtypeStruct((2, M), jnp.float32),
        ],
        scratch_shapes=[
            pltpu.VMEM((M // WIDTH, SD, WIDTH), jnp.float32),
            pltpu.VMEM((M // WIDTH, SD, WIDTH), jnp.int32),
            pltpu.SemaphoreType.DMA((2, M // WIDTH)),
        ],
        compiler_params=pltpu.CompilerParams(vmem_limit_bytes=16 << 20),
    )(dosages, called_mask)


def pack_kernel(place, scale, *refs, first, count):
    pieces, out = refs[:count], refs[-1]
    for which in range(count):
        away = pieces[which][:SD, :].astype(jnp.float32)
        centre = pieces[which][SD:, :].astype(jnp.float32)[0:1, :]
        value = (away + (centre - scale[0:1, :])) * scale[1:2, :]
        at = pl.multiple_of(place[SHARES + first + which] * SD, SD)
        out[pl.ds(at, SD), :] = jnp.where(away != 0.0, value, 0.0).astype(jnp.bfloat16)


def pack(pieces, first, place, scale, previous):
    count = len(pieces)
    given = [pltpu.with_memory_space_constraint(piece, pltpu.VMEM) for piece in pieces]
    if previous is not None:
        given.append(previous)
    out = pl.pallas_call(
        functools.partial(pack_kernel, first=first, count=count),
        in_specs=[pl.BlockSpec(memory_space=pltpu.SMEM)]
        + [pl.BlockSpec(memory_space=pltpu.VMEM)] * (1 + len(given)),
        out_specs=pl.BlockSpec(memory_space=pltpu.VMEM),
        out_shape=jax.ShapeDtypeStruct((N_ROW * SD, M), jnp.bfloat16),
        input_output_aliases={} if previous is None else {2 + count: 0},
        compiler_params=pltpu.CompilerParams(vmem_limit_bytes=16 << 20),
    )(place, scale, *given)
    return pltpu.with_memory_space_constraint(out, pltpu.VMEM)


def product_kernel(place, scale, piece, *refs, count, fresh):
    panels = refs[:count]
    out, panel_buf, wide, panel_sem = refs[count + (0 if fresh else 1) :]
    step = pl.program_id(0)

    def panel_copy(which, slot):
        return pltpu.make_async_copy(panels[which], panel_buf.at[slot], panel_sem.at[slot])

    @pl.when(step == 0)
    def _():
        panel_copy(0, 0).start()

    for which in range(1, count):

        @pl.when(step == which - 1)
        def _(which=which):
            panel_copy(which, which % 2).start()

    slot = step % 2
    panel_copy(0, slot).wait()

    centre = panel_buf[slot, SD:, :].astype(jnp.float32)[0:1, :]
    offset = centre - scale[0:1, :]
    away = panel_buf[slot, :SD, :].astype(jnp.float32)
    left = jnp.where(away != 0, away + offset, 0.0).astype(jnp.bfloat16)
    for a in range(N_ROW):
        part = lax.dot_general(
            left,
            piece[a * SD : (a + 1) * SD, :],
            (((1,), (1,)), ((), ())),
            preferred_element_type=jnp.float32,
        )
        wide[0, pl.ds(a, SD, stride=N_ROW), :] = part[:, :128]
        wide[1, pl.ds(a, SD, stride=N_ROW), :] = part[:, 128:]
    out[:, :, :128] = wide[0].reshape(SD, N_ROW, 128).astype(jnp.bfloat16)
    out[:, :, 128:] = wide[1].reshape(SD, N_ROW, 128).astype(jnp.bfloat16)


def products(panels, first, piece, place, scale, previous):
    count = len(panels)
    fresh = previous is None
    anywhere = pl.BlockSpec(memory_space=pl.ANY)
    return pl.pallas_call(
        functools.partial(product_kernel, count=count, fresh=fresh),
        grid_spec=pltpu.PrefetchScalarGridSpec(
            num_scalar_prefetch=1,
            grid=(count,),
            in_specs=[pl.BlockSpec((2, M), lambda i, place: (0, 0))]
            + [pl.BlockSpec(memory_space=pltpu.VMEM)]
            + [anywhere] * (count + (0 if fresh else 1)),
            out_specs=pl.BlockSpec((SD, N_ROW, SD), lambda i, place: (place[first + i], 0, 0)),
            scratch_shapes=[
                pltpu.VMEM((2, ROWS, M), jnp.bfloat16),
                pltpu.VMEM((2, SD * N_ROW, 128), jnp.float32),
                pltpu.SemaphoreType.DMA((2,)),
            ],
        ),
        out_shape=jax.ShapeDtypeStruct((SHARES * SD, N_ROW, SD), jnp.bfloat16),
        input_output_aliases={} if fresh else {3 + count: 0},
        compiler_params=pltpu.CompilerParams(vmem_limit_bytes=24 << 20),
        cost_estimate=pl.CostEstimate(
            flops=2 * count * SD * N_ROW * SD * M,
            bytes_accessed=2 * (count * SD * (M + N_ROW * SD) + N_ROW * SD * M),
            transcendentals=0,
        ),
    )(place, scale, piece, *panels, *([] if fresh else [previous]))


def steps(dosages, called_mask):
    own, sums = centred(
        pltpu.with_memory_space_constraint(dosages, pltpu.HBM),
        pltpu.with_memory_space_constraint(called_mask, pltpu.HBM),
    )
    sums = sums + swap(sums)
    for axis in (Y, X, Z):
        sums = ring_sum(sums, axis)
    frequency = sums[0] / (2.0 * jnp.maximum(sums[1], 1.0))
    spread = jnp.maximum(2.0 * frequency * (1.0 - frequency), 0.05)
    scale = jnp.stack([2.0 * frequency, (1.0 / M) / spread])

    line = {(0, 0): own}
    line[-1, 0] = shift(own, Y, 1)
    line[1, 0] = shift(own, Y, -1)
    line[0, 1] = swap(own)
    line[-1, 1] = swap(line[-1, 0])
    line[1, 1] = swap(line[1, 0])
    line[2, 0] = across(line[-1, 0], line[1, 0])
    line[2, 1] = swap(line[2, 0])

    plane = {(0, 0): own}
    for (dx, dz), axis, step in MOVES:
        target = (dx - step, dz) if axis == X else (dx, dz - step)
        plane[(target[0] + 1) % 4 - 1, (target[1] + 1) % 4 - 1] = shift(plane[dx, dz], axis, step)
    place = lax.dynamic_index_in_dim(
        jnp.asarray(places(list(plane), list(line))), lax.axis_index(ALL), keepdims=False
    )
    pieces = list(line.values())
    piece = pack(pieces[:6], 0, place, scale, None)
    piece = pack(pieces[6:], 6, place, scale, piece)
    shares = list(plane.values())
    total = None
    for first, last in CHUNKS:
        total = products(shares[first:last], first, piece, place, scale, total)
    return total.reshape(total.shape[0], N_ROW, 1, 1, SD)


MOVES = (
    ((0, 0), Z, 1),
    ((0, 0), Z, -1),
    ((0, 0), X, 1),
    ((0, 0), X, -1),
    ((0, -1), Z, 1),
    ((0, -1), X, 1),
    ((0, 1), X, -1),
    ((1, 0), Z, 1),
    ((-1, 0), Z, -1),
    ((-1, 0), X, 1),
    ((0, 2), X, -1),
    ((-1, 1), Z, -1),
    ((-1, -1), X, 1),
    ((1, 2), X, -1),
    ((2, 0), Z, -1),
)
CHUNKS = ((0, 5), (5, 11), (11, 16))


def solution(mesh):
    torus = Mesh(mesh.devices.reshape(4, 2, 4, 2, mesh.shape["half"]), ALL)
    return jax.shard_map(
        steps,
        mesh=torus,
        in_specs=(P(ALL, None), P(ALL, None)),
        out_specs=P(("row_0", "row_1"), None, ("col_0", "col_1"), "half", None),
        check_vma=False,
    )
```
